32 devices in a mesh: row: 8 (over z, x), col: 4 (over y, core).
Axes of the slice: x: 2, y: 2, z: 4, core: 2. Of those that a mesh axis runs over, the one named last changes fastest.
Arguments:
- coeffs: float32 [4096, 4096], P('row', 'col'), may hold values from -6 to 6
- ham_alpha: float32 [4096, 4096], P('row'), may hold values from -1.5 to 7.5, as said below
- ham_beta: float32 [4096, 4096], P('col'), may hold values from -1.5 to 7.5, as said below
Outputs:
- sigma_vec: float32 [4096, 4096], P('row', 'col')
The draws below stay inside these ranges and needn't reach their ends.
Inputs may be any that keep to these rules, and one draw needn't show every extreme that they name: `ham_alpha`: symmetric. `ham_beta`: symmetric.
All inputs are finite; a program needn't handle non-finite values.
Results may differ from the reference program's by a relative error of at most 0.00005.
Values sent between devices are 32-bit elements; how exact they have to be, the bound alone decides.
A program may use at most 128 MiB of HBM per device.

```python
import jax
import jax.numpy as jnp
from jax import lax

NSTR = 4096


def make_hamiltonian(key, which):
    folded = jax.random.fold_in(key, which)
    key_off, key_diag = jax.random.split(folded)
    normals = jax.random.truncated_normal(key_off, -6.0, 6.0, (NSTR, NSTR), jnp.float32)
    symmetric = (normals + normals.T) / jnp.sqrt(2.0 * NSTR)
    diagonal = jax.random.uniform(key_diag, (NSTR,), jnp.float32, 1.0, 3.0)
    return symmetric + jnp.diag(diagonal)


def draw_ham_alpha(key, part):
    return make_hamiltonian(key, 11)


def draw_ham_beta(key, part):
    return make_hamiltonian(key, 23)


def levels(key, extent, pieces, low, high):
    factor_of, own = 1.0, jax.random.fold_in(key, 6)
    for dim, blocks in pieces:
        draws = jnp.exp(jax.random.uniform(jax.random.fold_in(own, dim), (blocks,), jnp.float32, low / len(pieces), high / len(pieces)))
        factor_of = factor_of * jnp.repeat(draws, extent[dim] // blocks).reshape([-1 if axis == dim else 1 for axis in range(len(extent))])
    return factor_of


def scatter_about(stream_key, shape, scale, bound, shards=(), held_as=jnp.bfloat16):
    factor_of = levels(stream_key, shape, shards, -0.22, 0.18) if shards else 1.0
    entries = jax.random.normal(stream_key, shape, jnp.float32) * scale * factor_of
    return jnp.minimum(jnp.maximum(entries, -bound), bound).astype(held_as)


def setup_inputs(seed: int = 0) -> dict:
    streams_of = jax.random.split(jax.random.key(seed), 4)
    coeffs = scatter_about(streams_of[0], (NSTR, NSTR), 1.0, 6.0, ((0, 8), (1, 4)), jnp.float32)
    ham_alpha = draw_ham_alpha(jax.random.fold_in(streams_of[3], 71), 0)
    ham_beta = draw_ham_beta(jax.random.fold_in(streams_of[3], 71), 0)
    return dict(coeffs=coeffs, ham_alpha=ham_alpha, ham_beta=ham_beta)


def reference(coeffs, ham_alpha, ham_beta):
    alpha_part = jnp.dot(ham_alpha, coeffs, precision=lax.Precision.HIGHEST, preferred_element_type=jnp.float32)
    beta_part = jnp.dot(coeffs, ham_beta.T, precision=lax.Precision.HIGHEST, preferred_element_type=jnp.float32)
    return alpha_part + beta_part
```

```python
import functools

import jax
import jax.numpy as jnp
from jax import lax
from jax.experimental import pallas as pl
from jax.experimental.pallas import tpu as pltpu
from jax.sharding import PartitionSpec as P

PAIR = 2
LANES = 128
MESH = pl.DeviceIdType.MESH


def flip(index, key):
    bit = 1
    while bit <= key:
        if key & bit:
            index = index + bit - 2 * bit * ((index // bit) % 2)
        bit *= 2
    return index


def split(value):
    high = value.astype(jnp.bfloat16)
    return high, (value - high.astype(jnp.float32)).astype(jnp.bfloat16)


def product(lhs, rhs, lhs_dim, rhs_dim):
    lhs_high, lhs_low = split(lhs)
    rhs_high, rhs_low = split(rhs)

    def one(a, b):
        return lax.dot_general(
            a, b, (((lhs_dim,), (rhs_dim,)), ((), ())), preferred_element_type=jnp.float32
        )

    return one(lhs_high, rhs_high) + (one(lhs_high, rhs_low) + one(lhs_low, rhs_high))


def exchanges(n):
    held, mask, out = [0], n // 2, []
    while mask:
        out += [(mask, key) for key in held]
        held += [key ^ mask for key in held]
        mask //= 2
    return out


def kernel(
    line, cols_n, cw,
    coeffs, ha, hb, result,
    own, out, ham, beta, co, ag, rs, acc, acc_in, pair,
    l_sem, h_sem, b_sem, out_sem, a_send, a_recv, r_send, r_recv,
    x_send, x_recv, k_send, k_recv, o_send, o_recv, p_send, p_recv, c_send, c_recv,
):
    rows, cols = coeffs.shape
    nc = cols // 2 // cw
    units = cols // LANES
    prow = rows // cols_n
    tile = min(256, cols)
    row, col = lax.axis_index("row"), lax.axis_index("col")
    z, x = row // PAIR, row % PAIR
    partner = z * PAIR + 1 - x
    steps = exchanges(cols_n)
    masks = sorted({mask for mask, _ in steps}, reverse=True)
    groups = [[i for i, step in enumerate(steps) if step[0] == mask] for mask in masks]
    near = steps.index((1, 0))

    def lanes(c, width=cw):
        return pl.ds(pl.multiple_of(c * width, LANES), width)

    def sum_lanes(c):
        return pl.ds(pl.multiple_of((nc + c) * cw, LANES), cw)

    def place(f):
        return z + f * (line - 1 - 2 * z)

    def turn(index, f):
        return index + f * (line - 1 - 2 * index)

    side = (2 * z) // line
    low_z = z + side * (line - 1 - 2 * z)

    def slot(i):
        late = (i + low_z + 1) // line
        s = (1 - late) * (line - 1 - i) + late * (i - (line - 1 - low_z))
        return s + side * (line - 1 - 2 * s)

    def remote(src, dst, send, recv, to):
        return pltpu.make_async_remote_copy(
            src_ref=src, dst_ref=dst, send_sem=send, recv_sem=recv,
            device_id=to, device_id_type=MESH,
        )

    def own_load():
        return pltpu.make_async_copy(coeffs, own, l_sem.at[0])

    def pair_load():
        return pltpu.make_async_copy(
            coeffs.at[:, pl.ds(nc * cw, nc * cw)], pair.at[0], l_sem.at[1]
        )

    def ham_load(s):
        at = pl.multiple_of((s * PAIR + x) * rows, LANES)
        return pltpu.make_async_copy(ha.at[:, pl.ds(at, rows)], ham.at[0, s], h_sem.at[s])

    def beta_load(key):
        at = pl.multiple_of(flip(col, key) * cols, LANES)
        return pltpu.make_async_copy(hb.at[:, pl.ds(at, cols)], beta.at[key], b_sem.at[key])

    own_load().start()
    beta_load(0).start()
    for s in range(line):
        ham_load(s).start()
    pair_load().start()
    for key in range(1, cols_n):
        beta_load(key).start()

    barrier = pltpu.get_barrier_semaphore()
    has_low, has_high = z > 0, z < line - 1

    def greet(to):
        pl.semaphore_signal(barrier, inc=1, device_id=to, device_id_type=MESH)

    greet((partner, col))
    for mask in masks:
        greet((row, flip(col, mask)))

    @pl.when(has_low)
    def _():
        greet((row - PAIR, col))

    @pl.when(has_high)
    def _():
        greet((row + PAIR, col))

    inner = jnp.logical_and(has_low, has_high)

    @pl.when(inner)
    def _():
        pl.semaphore_wait(barrier, 3 + len(masks))

    @pl.when(jnp.logical_not(inner))
    def _():
        pl.semaphore_wait(barrier, 2 + len(masks))

    def onward(f):
        return (row + PAIR - 2 * PAIR * f, col)

    def gather_copy(f, j, c):
        src = coeffs.at[:, lanes(c)] if isinstance(j, int) and j == 0 else ag.at[f, j - 1, :, lanes(c)]
        return remote(
            src, ag.at[f, j, :, lanes(c)], a_send.at[f, j, c], a_recv.at[f, j, c], onward(f)
        )

    def sum_copy(f, j, c):
        return remote(
            rs.at[f, j - 1, :, lanes(c)], rs.at[f, j, :, lanes(c)],
            r_send.at[f, j, c], r_recv.at[f, j, c], onward(f),
        )

    def goes_on(f):
        return place(f) < line - 1

    def piece(i, index):
        return ham.at[1, slot(i), pl.ds(pl.multiple_of(index * prow, 8), prow)]

    def piece_copy(i):
        at = pl.multiple_of((slot(i) * PAIR + 1 - x) * rows, LANES)
        src = ha.at[pl.ds(pl.multiple_of(col * prow, 8), prow), pl.ds(at, rows)]
        return remote(src, piece(i, col), x_send.at[i], x_recv.at[i], (partner, col))

    def pair_copy(c):
        return remote(
            coeffs.at[:, sum_lanes(c)], pair.at[1, :, lanes(c)],
            k_send.at[c], k_recv.at[c], (partner, col),
        )

    def other_copy(c):
        return remote(
            acc.at[1, :, lanes(c)], acc_in.at[:, lanes(c)], o_send.at[c], o_recv.at[c],
            (partner, col),
        )

    def p_copy(n, i):
        mask, key = steps[n]
        part = piece(i, flip(col, key))
        return remote(part, part, p_send.at[n, i], p_recv.at[n, i], (row, flip(col, mask)))

    def p_got(n, i):
        mask, key = steps[n]
        part = piece(i, flip(col, key ^ mask))
        return remote(part, part, p_send.at[n, i], p_recv.at[n, i], (row, flip(col, mask)))

    def c_copy(n, u):
        mask, key = steps[n]
        at = lanes(u, LANES)
        src = coeffs.at[:, at] if key == 0 else co.at[key - 1, :, at]
        return remote(
            src, co.at[(key ^ mask) - 1, :, at], c_send.at[n, u], c_recv.at[n, u],
            (row, flip(col, mask)),
        )

    @pl.when(has_high)
    def _():
        for c in range(nc):
            gather_copy(0, 0, c).start()

    @pl.when(has_low)
    def _():
        for c in range(nc):
            gather_copy(1, 0, c).start()

    piece_copy(0).start()
    c_copy(groups[0][0], 0).start()
    for c in range(nc):
        pair_copy(c).start()
    for i in range(1, line):
        piece_copy(i).start()
    for group in groups[1:]:
        for u in range(units):
            c_copy(group[0], u).start()

    def pass_piece(i):
        piece_copy(i).wait_recv()
        for group in groups:
            p_copy(group[0], i).start()

    def have_piece(i):
        for g, group in enumerate(groups):
            if g:
                for n in group[1:]:
                    p_copy(n, i).start()
            for n in group:
                p_got(n, i).wait_recv()

    def have_units(first, last):
        for g, group in enumerate(groups):
            if g:
                for u in range(first, last):
                    for n in group[1:]:
                        c_copy(n, u).start()
            for u in range(first, last):
                for n in group:
                    if n != near:
                        c_copy(n, u).wait_recv()

    def add_beta(key, add, k_at=0, k_width=cols):
        depth = pl.ds(k_at, k_width)
        lhs = own if key == 0 else co.at[key - 1]

        @pl.loop(0, cols // tile)
        def _(n):
            at = lanes(n, tile)
            value = product(lhs[:, depth], beta[key, at, depth], 1, 1)
            out[:, at] = out[:, at] + value if add else value

    def term(d, c):
        def one(m):
            return product(ham[m, d], pair[m, :, lanes(c)], 0, 0)

        return one(0) + one(1)

    def add_gathered(m, s, f, b, c):
        at = lanes(c)
        acc[m, :, at] = acc[m, :, at] + product(ham[m, s], ag[f, b, :, at], 1, 0)

    own_load().wait()
    beta_load(0).wait()
    add_beta(0, False)
    pass_piece(0)
    for u in range(1, units // 2 + 1):
        c_copy(groups[0][0], u).start()

    for s in range(line):
        ham_load(s).wait()
    pair_load().wait()

    @pl.loop(0, nc)
    def _(c):
        acc[0, :, lanes(c)] = product(ham[0, z], own[:, lanes(c)], 1, 0)

    for key in range(1, cols_n):
        beta_load(key).wait()
    for u in range(units):
        c_copy(near, u).wait_recv()
    add_beta(1, True)
    have_piece(0)

    def second_products(c):
        at = lanes(c)
        acc[1, :, at] = product(ham[1, z], own[:, at], 1, 0)

        @pl.loop(0, 2)
        def _(f):
            for b in range(2):
                @pl.when(b < place(f))
                def _(b=b):
                    add_gathered(1, turn(place(f) - 1 - b, f), f, b, c)

    for j in range(1, line):
        if j == 2:
            pass_piece(1)
            have_units(0, units // 2)
            for key in range(2, cols_n):
                add_beta(key, True, 0, cols // 2)
            have_piece(1)

        @pl.loop(0, nc)
        def _(c, j=j):
            if j == 2:
                @pl.when(c + 2 < line)
                def _():
                    pass_piece(c + 2)

            if j == 1:
                pair_copy(c).wait_recv()

            @pl.loop(0, 2)
            def _(f):
                at = place(f)

                @pl.when(at >= j)
                def _():
                    gather_copy(f, j - 1, c).wait_recv()

                    if j < line - 1:
                        @pl.when(goes_on(f))
                        def _():
                            gather_copy(f, j, c).start()

                @pl.when(jnp.logical_and(at < j, goes_on(f)))
                def _():
                    value = term(turn(line + at - j, f), c)
                    if j == 1:
                        rs[f, j - 1, :, lanes(c)] = value
                    else:
                        @pl.when(at > 0)
                        def _():
                            sum_copy(f, j - 1, c).wait_recv()
                            rs[f, j - 1, :, lanes(c)] = rs[f, j - 1, :, lanes(c)] + value

                        @pl.when(at == 0)
                        def _():
                            rs[f, j - 1, :, lanes(c)] = value

                    sum_copy(f, j, c).start()

            if j == 3:
                second_products(c)

            @pl.loop(0, 2)
            def _(f):
                at = place(f)

                @pl.when(at >= j)
                def _():
                    @pl.loop(0, 1 if j < 3 else PAIR)
                    def _(m):
                        add_gathered(m, turn(at - j, f), f, j - 1, c)

            if j == line - 1:
                other_copy(c).start()

        if j == 2:
            for i in range(nc + 2, line):
                pass_piece(i)
            for u in range(units // 2 + 1, units):
                c_copy(groups[0][0], u).start()
            for i in range(2, line):
                have_piece(i)

    have_units(units // 2, units)
    for key in range(2, cols_n):
        add_beta(key, True, cols // 2, cols // 2)

    @pl.loop(0, nc)
    def _(c):
        at = sum_lanes(c)
        out[:, at] = out[:, at] + term(z, c)

    def out_copy(at, n):
        return pltpu.make_async_copy(out.at[:, at], result.at[:, at], out_sem.at[n])

    def finish_sums(c):
        at = sum_lanes(c)

        @pl.loop(0, 2)
        def _(f):
            @pl.when(place(f) > 0)
            def _():
                sum_copy(f, line - 1, c).wait_recv()
                out[:, at] = out[:, at] + rs[f, line - 1, :, lanes(c)]

        out_copy(at, nc + c).start()

    def finish_gathered(c):
        at = lanes(c)
        other_copy(c).wait_recv()
        out[:, at] = out[:, at] + (acc[0, :, at] + acc_in[:, at])
        out_copy(at, c).start()

    @pl.loop(0, nc - 1)
    def _(c):
        finish_sums(c)

    @pl.loop(0, nc)
    def _(c):
        finish_gathered(c)

    finish_sums(nc - 1)

    for i in range(line):
        piece_copy(i).wait_send()
        for n in range(len(steps)):
            p_copy(n, i).wait_send()
    for u in range(units):
        for n in range(len(steps)):
            c_copy(n, u).wait_send()
    for c in range(nc):
        pair_copy(c).wait_send()
        other_copy(c).wait_send()

    @pl.loop(0, 2)
    def _(f):
        @pl.when(goes_on(f))
        def _():
            @pl.loop(0, nc)
            def _(c):
                for j in range(line):
                    if j < line - 1:
                        @pl.when(j <= place(f))
                        def _(j=j):
                            gather_copy(f, j, c).wait_send()

                    if j:
                        @pl.when(j > place(f))
                        def _(j=j):
                            sum_copy(f, j, c).wait_send()

    for n in range(nc):
        out_copy(lanes(n), n).wait()
        out_copy(sum_lanes(n), nc + n).wait()


def solution(mesh):
    line, cols_n = mesh.shape["row"] // PAIR, mesh.shape["col"]
    n_steps = len(exchanges(cols_n))

    def local(coeffs, ham_alpha, ham_beta):
        rows, cols = coeffs.shape
        half = cols // 2
        cw = min(256, half)
        nc = half // cw
        units = cols // LANES
        f32, dma = jnp.float32, pltpu.SemaphoreType.DMA
        any_spec = pl.BlockSpec(memory_space=pl.ANY)
        return pl.pallas_call(
            functools.partial(kernel, line, cols_n, cw),
            out_shape=jax.ShapeDtypeStruct((rows, cols), f32),
            in_specs=[any_spec, any_spec, any_spec],
            out_specs=any_spec,
            scratch_shapes=[
                pltpu.VMEM((rows, cols), f32),
                pltpu.VMEM((rows, cols), f32),
                pltpu.VMEM((PAIR, line, rows, rows), f32),
                pltpu.VMEM((cols_n, cols, cols), f32),
                pltpu.VMEM((cols_n - 1, rows, cols), f32),
                pltpu.VMEM((2, line - 1, rows, half), f32),
                pltpu.VMEM((2, line, rows, half), f32),
                pltpu.VMEM((PAIR, rows, half), f32),
                pltpu.VMEM((rows, half), f32),
                pltpu.VMEM((PAIR, rows, half), f32),
                dma((2,)),
                dma((line,)),
                dma((cols_n,)),
                dma((2 * nc,)),
                dma((2, line - 1, nc)),
                dma((2, line - 1, nc)),
                dma((2, line, nc)),
                dma((2, line, nc)),
                dma((line,)),
                dma((line,)),
                dma((nc,)),
                dma((nc,)),
                dma((nc,)),
                dma((nc,)),
                dma((n_steps, line)),
                dma((n_steps, line)),
                dma((n_steps, units)),
                dma((n_steps, units)),
            ],
            compiler_params=pltpu.CompilerParams(
                collective_id=0, has_side_effects=True, vmem_limit_bytes=67043328
            ),
        )(coeffs, ham_alpha, ham_beta)

    in_specs = (P("row", "col"), P("row", None), P("col", None))
    return jax.shard_map(
        local, mesh=mesh, in_specs=in_specs, out_specs=P("row", "col"), check_vma=False
    )
```

```python
import functools

import jax
import jax.numpy as jnp
from jax import lax
from jax.experimental import pallas as pl
from jax.experimental.pallas import tpu as pltpu
from jax.sharding import PartitionSpec as P

PAIR = 2
LANES = 128
MESH = pl.DeviceIdType.MESH


def flip(index, key):
    bit = 1
    while bit <= key:
        if key & bit:
            index = index + bit - 2 * bit * ((index // bit) % 2)
        bit *= 2
    return index


def split(value):
    high = value.astype(jnp.bfloat16)
    return high, (value - high.astype(jnp.float32)).astype(jnp.bfloat16)


def product(lhs, rhs, lhs_dim, rhs_dim):
    lhs_high, lhs_low = split(lhs)
    rhs_high, rhs_low = split(rhs)

    def one(a, b):
        return lax.dot_general(
            a, b, (((lhs_dim,), (rhs_dim,)), ((), ())), preferred_element_type=jnp.float32
        )

    return one(lhs_high, rhs_high) + (one(lhs_high, rhs_low) + one(lhs_low, rhs_high))


def exchanges(n):
    held, mask, out = [0], n // 2, []
    while mask:
        out += [(mask, key) for key in held]
        held += [key ^ mask for key in held]
        mask //= 2
    return out


def kernel(
    line, cols_n, cw,
    coeffs, ha, hb, out,
    own, ham, beta, co, ag, rs, acc, acc_in, pair,
    l_sem, h_sem, b_sem, a_send, a_recv, r_send, r_recv,
    x_send, x_recv, k_send, k_recv, o_send, o_recv, p_send, p_recv, c_send, c_recv,
):
    rows, cols = coeffs.shape
    nc = cols // 2 // cw
    units = cols // LANES
    prow = rows // cols_n
    tile = min(256, cols)
    row, col = lax.axis_index("row"), lax.axis_index("col")
    z, x = row // PAIR, row % PAIR
    partner = z * PAIR + 1 - x
    steps = exchanges(cols_n)
    masks = sorted({mask for mask, _ in steps}, reverse=True)
    groups = [[i for i, step in enumerate(steps) if step[0] == mask] for mask in masks]
    near = steps.index((1, 0))

    def lanes(c, width=cw):
        return pl.ds(pl.multiple_of(c * width, LANES), width)

    def sum_lanes(c):
        return pl.ds(pl.multiple_of((nc + c) * cw, LANES), cw)

    def place(f):
        return z + f * (line - 1 - 2 * z)

    def turn(index, f):
        return index + f * (line - 1 - 2 * index)

    side = (2 * z) // line
    low_z = z + side * (line - 1 - 2 * z)

    def slot(i):
        late = (i + low_z + 1) // line
        s = (1 - late) * (line - 1 - i) + late * (i - (line - 1 - low_z))
        return s + side * (line - 1 - 2 * s)

    def remote(src, dst, send, recv, to):
        return pltpu.make_async_remote_copy(
            src_ref=src, dst_ref=dst, send_sem=send, recv_sem=recv,
            device_id=to, device_id_type=MESH,
        )

    def own_load():
        return pltpu.make_async_copy(coeffs, own, l_sem.at[0])

    def pair_load():
        return pltpu.make_async_copy(
            coeffs.at[:, pl.ds(nc * cw, nc * cw)], pair.at[0], l_sem.at[1]
        )

    def ham_load(s):
        at = pl.multiple_of((s * PAIR + x) * rows, LANES)
        return pltpu.make_async_copy(ha.at[:, pl.ds(at, rows)], ham.at[0, s], h_sem.at[s])

    def beta_load(key):
        at = pl.multiple_of(flip(col, key) * cols, LANES)
        return pltpu.make_async_copy(hb.at[:, pl.ds(at, cols)], beta.at[key], b_sem.at[key])

    own_load().start()
    beta_load(0).start()
    for s in range(line):
        ham_load(s).start()
    pair_load().start()
    for key in range(1, cols_n):
        beta_load(key).start()

    barrier = pltpu.get_barrier_semaphore()
    has_low, has_high = z > 0, z < line - 1

    def greet(to):
        pl.semaphore_signal(barrier, inc=1, device_id=to, device_id_type=MESH)

    greet((partner, col))
    for mask in masks:
        greet((row, flip(col, mask)))

    @pl.when(has_low)
    def _():
        greet((row - PAIR, col))

    @pl.when(has_high)
    def _():
        greet((row + PAIR, col))

    inner = jnp.logical_and(has_low, has_high)

    @pl.when(inner)
    def _():
        pl.semaphore_wait(barrier, 3 + len(masks))

    @pl.when(jnp.logical_not(inner))
    def _():
        pl.semaphore_wait(barrier, 2 + len(masks))

    def onward(f):
        return (row + PAIR - 2 * PAIR * f, col)

    def gather_copy(f, j, c):
        src = coeffs.at[:, lanes(c)] if isinstance(j, int) and j == 0 else ag.at[f, j - 1, :, lanes(c)]
        return remote(
            src, ag.at[f, j, :, lanes(c)], a_send.at[f, j, c], a_recv.at[f, j, c], onward(f)
        )

    def sum_copy(f, j, c):
        return remote(
            rs.at[f, j - 1, :, lanes(c)], rs.at[f, j, :, lanes(c)],
            r_send.at[f, j, c], r_recv.at[f, j, c], onward(f),
        )

    def goes_on(f):
        return place(f) < line - 1

    def piece(i, index):
        return ham.at[1, slot(i), pl.ds(pl.multiple_of(index * prow, 8), prow)]

    def piece_copy(i):
        at = pl.multiple_of((slot(i) * PAIR + 1 - x) * rows, LANES)
        src = ha.at[pl.ds(pl.multiple_of(col * prow, 8), prow), pl.ds(at, rows)]
        return remote(src, piece(i, col), x_send.at[i], x_recv.at[i], (partner, col))

    def pair_copy(c):
        return remote(
            coeffs.at[:, sum_lanes(c)], pair.at[1, :, lanes(c)],
            k_send.at[c], k_recv.at[c], (partner, col),
        )

    def other_copy(c):
        return remote(
            acc.at[1, :, lanes(c)], acc_in.at[:, lanes(c)], o_send.at[c], o_recv.at[c],
            (partner, col),
        )

    def p_copy(n, i):
        mask, key = steps[n]
        part = piece(i, flip(col, key))
        return remote(part, part, p_send.at[n, i], p_recv.at[n, i], (row, flip(col, mask)))

    def p_got(n, i):
        mask, key = steps[n]
        part = piece(i, flip(col, key ^ mask))
        return remote(part, part, p_send.at[n, i], p_recv.at[n, i], (row, flip(col, mask)))

    def c_copy(n, u):
        mask, key = steps[n]
        at = lanes(u, LANES)
        src = coeffs.at[:, at] if key == 0 else co.at[key - 1, :, at]
        return remote(
            src, co.at[(key ^ mask) - 1, :, at], c_send.at[n, u], c_recv.at[n, u],
            (row, flip(col, mask)),
        )

    @pl.when(has_high)
    def _():
        for c in range(nc):
            gather_copy(0, 0, c).start()

    @pl.when(has_low)
    def _():
        for c in range(nc):
            gather_copy(1, 0, c).start()

    piece_copy(0).start()
    c_copy(groups[0][0], 0).start()
    for c in range(nc):
        pair_copy(c).start()
    for i in range(1, line):
        piece_copy(i).start()
    for group in groups[1:]:
        for u in range(units):
            c_copy(group[0], u).start()

    def pass_piece(i):
        piece_copy(i).wait_recv()
        for group in groups:
            p_copy(group[0], i).start()

    def have_piece(i):
        for g, group in enumerate(groups):
            if g:
                for n in group[1:]:
                    p_copy(n, i).start()
            for n in group:
                p_got(n, i).wait_recv()

    def have_units(first, last):
        for g, group in enumerate(groups):
            if g:
                for u in range(first, last):
                    for n in group[1:]:
                        c_copy(n, u).start()
            for u in range(first, last):
                for n in group:
                    if n != near:
                        c_copy(n, u).wait_recv()

    def add_beta(key, add, k_at=0, k_width=cols):
        depth = pl.ds(k_at, k_width)
        lhs = own if key == 0 else co.at[key - 1]

        @pl.loop(0, cols // tile)
        def _(n):
            at = lanes(n, tile)
            value = product(lhs[:, depth], beta[key, at, depth], 1, 1)
            out[:, at] = out[:, at] + value if add else value

    def term(d, c):
        def one(m):
            return product(ham[m, d], pair[m, :, lanes(c)], 0, 0)

        return one(0) + one(1)

    def add_gathered(m, s, f, b, c):
        at = lanes(c)
        acc[m, :, at] = acc[m, :, at] + product(ham[m, s], ag[f, b, :, at], 1, 0)

    own_load().wait()
    beta_load(0).wait()
    add_beta(0, False)
    pass_piece(0)
    for u in range(1, units // 2 + 1):
        c_copy(groups[0][0], u).start()

    for s in range(line):
        ham_load(s).wait()
    pair_load().wait()

    @pl.loop(0, nc)
    def _(c):
        acc[0, :, lanes(c)] = product(ham[0, z], own[:, lanes(c)], 1, 0)

    for key in range(1, cols_n):
        beta_load(key).wait()
    for u in range(units):
        c_copy(near, u).wait_recv()
    add_beta(1, True)
    have_piece(0)

    def second_products(c):
        at = lanes(c)
        acc[1, :, at] = product(ham[1, z], own[:, at], 1, 0)

        @pl.loop(0, 2)
        def _(f):
            for b in range(2):
                @pl.when(b < place(f))
                def _(b=b):
                    add_gathered(1, turn(place(f) - 1 - b, f), f, b, c)

    for j in range(1, line):
        if j == 2:
            pass_piece(1)
            have_units(0, units // 2)
            for key in range(2, cols_n):
                add_beta(key, True, 0, cols // 2)
            have_piece(1)

        @pl.loop(0, nc)
        def _(c, j=j):
            if j == 2:
                @pl.when(c + 2 < line)
                def _():
                    pass_piece(c + 2)

            if j == 1:
                pair_copy(c).wait_recv()

            @pl.loop(0, 2)
            def _(f):
                at = place(f)

                @pl.when(at >= j)
                def _():
                    gather_copy(f, j - 1, c).wait_recv()

                    if j < line - 1:
                        @pl.when(goes_on(f))
                        def _():
                            gather_copy(f, j, c).start()

                @pl.when(jnp.logical_and(at < j, goes_on(f)))
                def _():
                    value = term(turn(line + at - j, f), c)
                    if j == 1:
                        rs[f, j - 1, :, lanes(c)] = value
                    else:
                        @pl.when(at > 0)
                        def _():
                            sum_copy(f, j - 1, c).wait_recv()
                            rs[f, j - 1, :, lanes(c)] = rs[f, j - 1, :, lanes(c)] + value

                        @pl.when(at == 0)
                        def _():
                            rs[f, j - 1, :, lanes(c)] = value

                    sum_copy(f, j, c).start()

            if j == 3:
                second_products(c)

            @pl.loop(0, 2)
            def _(f):
                at = place(f)

                @pl.when(at >= j)
                def _():
                    @pl.loop(0, 1 if j < 3 else PAIR)
                    def _(m):
                        add_gathered(m, turn(at - j, f), f, j - 1, c)

            if j == line - 1:
                other_copy(c).start()

        if j == 2:
            for i in range(nc + 2, line):
                pass_piece(i)
            for u in range(units // 2 + 1, units):
                c_copy(groups[0][0], u).start()
            for i in range(2, line):
                have_piece(i)

    have_units(units // 2, units)
    for key in range(2, cols_n):
        add_beta(key, True, cols // 2, cols // 2)

    @pl.loop(0, nc)
    def _(c):
        at = sum_lanes(c)
        out[:, at] = out[:, at] + term(z, c)

    def finish_sums(c):
        at = sum_lanes(c)

        @pl.loop(0, 2)
        def _(f):
            @pl.when(place(f) > 0)
            def _():
                sum_copy(f, line - 1, c).wait_recv()
                out[:, at] = out[:, at] + rs[f, line - 1, :, lanes(c)]

    def finish_gathered(c):
        at = lanes(c)
        other_copy(c).wait_recv()
        out[:, at] = out[:, at] + (acc[0, :, at] + acc_in[:, at])

    @pl.loop(0, nc - 1)
    def _(c):
        finish_sums(c)

    @pl.loop(0, nc)
    def _(c):
        finish_gathered(c)

    finish_sums(nc - 1)

    for i in range(line):
        piece_copy(i).wait_send()
        for n in range(len(steps)):
            p_copy(n, i).wait_send()
    for u in range(units):
        for n in range(len(steps)):
            c_copy(n, u).wait_send()
    for c in range(nc):
        pair_copy(c).wait_send()
        other_copy(c).wait_send()

    @pl.loop(0, 2)
    def _(f):
        @pl.when(goes_on(f))
        def _():
            @pl.loop(0, nc)
            def _(c):
                for j in range(line):
                    if j < line - 1:
                        @pl.when(j <= place(f))
                        def _(j=j):
                            gather_copy(f, j, c).wait_send()

                    if j:
                        @pl.when(j > place(f))
                        def _(j=j):
                            sum_copy(f, j, c).wait_send()


def solution(mesh):
    line, cols_n = mesh.shape["row"] // PAIR, mesh.shape["col"]
    n_steps = len(exchanges(cols_n))

    def local(coeffs, ham_alpha, ham_beta):
        rows, cols = coeffs.shape
        half = cols // 2
        cw = min(256, half)
        nc = half // cw
        units = cols // LANES
        f32, dma = jnp.float32, pltpu.SemaphoreType.DMA
        any_spec = pl.BlockSpec(memory_space=pl.ANY)
        return pl.pallas_call(
            functools.partial(kernel, line, cols_n, cw),
            out_shape=pltpu.VMEM((rows, cols), f32),
            in_specs=[any_spec, any_spec, any_spec],
            out_specs=pl.BlockSpec(memory_space=pltpu.VMEM),
            scratch_shapes=[
                pltpu.VMEM((rows, cols), f32),
                pltpu.VMEM((PAIR, line, rows, rows), f32),
                pltpu.VMEM((cols_n, cols, cols), f32),
                pltpu.VMEM((cols_n - 1, rows, cols), f32),
                pltpu.VMEM((2, line - 1, rows, half), f32),
                pltpu.VMEM((2, line, rows, half), f32),
                pltpu.VMEM((PAIR, rows, half), f32),
                pltpu.VMEM((rows, half), f32),
                pltpu.VMEM((PAIR, rows, half), f32),
                dma((2,)),
                dma((line,)),
                dma((cols_n,)),
                dma((2, line - 1, nc)),
                dma((2, line - 1, nc)),
                dma((2, line, nc)),
                dma((2, line, nc)),
                dma((line,)),
                dma((line,)),
                dma((nc,)),
                dma((nc,)),
                dma((nc,)),
                dma((nc,)),
                dma((n_steps, line)),
                dma((n_steps, line)),
                dma((n_steps, units)),
                dma((n_steps, units)),
            ],
            compiler_params=pltpu.CompilerParams(
                collective_id=0, has_side_effects=True, vmem_limit_bytes=58 * 2**20
            ),
        )(coeffs, ham_alpha, ham_beta)

    in_specs = (P("row", "col"), P("row", None), P("col", None))
    return jax.shard_map(
        local, mesh=mesh, in_specs=in_specs, out_specs=P("row", "col"), check_vma=False
    )
```

```python
import functools

import jax
import jax.numpy as jnp
from jax import lax
from jax.experimental import pallas as pl
from jax.experimental.pallas import tpu as pltpu
from jax.sharding import PartitionSpec as P

PAIR = 2
LANES = 128
MESH = pl.DeviceIdType.MESH


def flip(index, key):
    bit = 1
    while bit <= key:
        if key & bit:
            index = index + bit - 2 * bit * ((index // bit) % 2)
        bit *= 2
    return index


def split(value):
    high = value.astype(jnp.bfloat16)
    return high, (value - high.astype(jnp.float32)).astype(jnp.bfloat16)


def product(lhs, rhs, lhs_dim, rhs_dim):
    lhs_high, lhs_low = split(lhs)
    rhs_high, rhs_low = split(rhs)

    def one(a, b):
        return lax.dot_general(
            a, b, (((lhs_dim,), (rhs_dim,)), ((), ())), preferred_element_type=jnp.float32
        )

    return one(lhs_high, rhs_high) + (one(lhs_high, rhs_low) + one(lhs_low, rhs_high))


def exchanges(n):
    held, mask, out = [0], n // 2, []
    while mask:
        out += [(mask, key) for key in held]
        held += [key ^ mask for key in held]
        mask //= 2
    return out


def kernel(
    line, cols_n, cw,
    coeffs, ha, hb, out,
    own, ham, beta, co, ag, rs, acc, acc_in, pair,
    l_sem, h_sem, b_sem, a_send, a_recv, r_send, r_recv,
    x_send, x_recv, k_send, k_recv, o_send, o_recv, p_send, p_recv, c_send, c_recv,
):
    rows, cols = coeffs.shape
    nc = cols // 2 // cw
    units = cols // LANES
    prow = rows // cols_n
    tile = min(256, cols)
    row, col = lax.axis_index("row"), lax.axis_index("col")
    z, x = row // PAIR, row % PAIR
    partner = z * PAIR + 1 - x
    steps = exchanges(cols_n)
    masks = sorted({mask for mask, _ in steps}, reverse=True)
    groups = [[i for i, step in enumerate(steps) if step[0] == mask] for mask in masks]
    near = steps.index((1, 0))

    def lanes(c, width=cw):
        return pl.ds(pl.multiple_of(c * width, LANES), width)

    def sum_lanes(c):
        return pl.ds(pl.multiple_of((nc + c) * cw, LANES), cw)

    def place(f):
        return z + f * (line - 1 - 2 * z)

    def turn(index, f):
        return index + f * (line - 1 - 2 * index)

    side = (2 * z) // line
    low_z = z + side * (line - 1 - 2 * z)

    def slot(i):
        late = (i + low_z + 1) // line
        s = (1 - late) * (line - 1 - i) + late * (i - (line - 1 - low_z))
        return s + side * (line - 1 - 2 * s)

    def remote(src, dst, send, recv, to):
        return pltpu.make_async_remote_copy(
            src_ref=src, dst_ref=dst, send_sem=send, recv_sem=recv,
            device_id=to, device_id_type=MESH,
        )

    def own_load():
        return pltpu.make_async_copy(coeffs, own, l_sem.at[0])

    def pair_load():
        return pltpu.make_async_copy(
            coeffs.at[:, pl.ds(nc * cw, nc * cw)], pair.at[0], l_sem.at[1]
        )

    def ham_load(s):
        at = pl.multiple_of((s * PAIR + x) * rows, LANES)
        return pltpu.make_async_copy(ha.at[:, pl.ds(at, rows)], ham.at[0, s], h_sem.at[s])

    def beta_load(key):
        at = pl.multiple_of(flip(col, key) * cols, LANES)
        return pltpu.make_async_copy(hb.at[:, pl.ds(at, cols)], beta.at[key], b_sem.at[key])

    own_load().start()
    beta_load(0).start()
    for s in range(line):
        ham_load(s).start()
    pair_load().start()
    for key in range(1, cols_n):
        beta_load(key).start()

    barrier = pltpu.get_barrier_semaphore()
    has_low, has_high = z > 0, z < line - 1

    def greet(to):
        pl.semaphore_signal(barrier, inc=1, device_id=to, device_id_type=MESH)

    greet((partner, col))
    for mask in masks:
        greet((row, flip(col, mask)))

    @pl.when(has_low)
    def _():
        greet((row - PAIR, col))

    @pl.when(has_high)
    def _():
        greet((row + PAIR, col))

    inner = jnp.logical_and(has_low, has_high)

    @pl.when(inner)
    def _():
        pl.semaphore_wait(barrier, 3 + len(masks))

    @pl.when(jnp.logical_not(inner))
    def _():
        pl.semaphore_wait(barrier, 2 + len(masks))

    def onward(f):
        return (row + PAIR - 2 * PAIR * f, col)

    def gather_copy(f, j, c):
        src = coeffs.at[:, lanes(c)] if isinstance(j, int) and j == 0 else ag.at[f, j - 1, :, lanes(c)]
        return remote(
            src, ag.at[f, j, :, lanes(c)], a_send.at[f, j, c], a_recv.at[f, j, c], onward(f)
        )

    def sum_copy(f, j, c):
        return remote(
            rs.at[f, j - 1, :, lanes(c)], rs.at[f, j, :, lanes(c)],
            r_send.at[f, j, c], r_recv.at[f, j, c], onward(f),
        )

    def goes_on(f):
        return place(f) < line - 1

    def share(i):
        return (rows // 2, 2) if isinstance(i, int) and i == 1 else (prow, cols_n)

    def piece_rows(i, index):
        height, n = share(i)
        return pl.ds(pl.multiple_of(index % n * height, 8), height)

    def piece(i, index):
        return ham.at[1, slot(i), piece_rows(i, index)]

    def hops(i):
        return [[near]] if isinstance(i, int) and i == 1 else groups

    def piece_copy(i):
        at = pl.multiple_of((slot(i) * PAIR + 1 - x) * rows, LANES)
        src = ha.at[piece_rows(i, col), pl.ds(at, rows)]
        return remote(src, piece(i, col), x_send.at[i], x_recv.at[i], (partner, col))

    def pair_copy(c):
        return remote(
            coeffs.at[:, sum_lanes(c)], pair.at[1, :, lanes(c)],
            k_send.at[c], k_recv.at[c], (partner, col),
        )

    def other_copy(c):
        return remote(
            acc.at[1, :, lanes(c)], acc_in.at[:, lanes(c)], o_send.at[c], o_recv.at[c],
            (partner, col),
        )

    def p_copy(n, i):
        mask, key = steps[n]
        part = piece(i, flip(col, key))
        return remote(part, part, p_send.at[n, i], p_recv.at[n, i], (row, flip(col, mask)))

    def p_got(n, i):
        mask, key = steps[n]
        part = piece(i, flip(col, key ^ mask))
        return remote(part, part, p_send.at[n, i], p_recv.at[n, i], (row, flip(col, mask)))

    def c_copy(n, u):
        mask, key = steps[n]
        at = lanes(u, LANES)
        src = coeffs.at[:, at] if key == 0 else co.at[key - 1, :, at]
        return remote(
            src, co.at[(key ^ mask) - 1, :, at], c_send.at[n, u], c_recv.at[n, u],
            (row, flip(col, mask)),
        )

    @pl.when(has_high)
    def _():
        for c in range(nc):
            gather_copy(0, 0, c).start()

    @pl.when(has_low)
    def _():
        for c in range(nc):
            gather_copy(1, 0, c).start()

    piece_copy(0).start()
    c_copy(groups[0][0], 0).start()
    for c in range(nc):
        pair_copy(c).start()
    for i in range(1, line):
        piece_copy(i).start()
    for group in groups[1:]:
        for u in range(units):
            c_copy(group[0], u).start()

    def pass_piece(i):
        piece_copy(i).wait_recv()
        for group in hops(i):
            p_copy(group[0], i).start()

    def have_piece(i):
        for g, group in enumerate(hops(i)):
            if g:
                for n in group[1:]:
                    p_copy(n, i).start()
            for n in group:
                p_got(n, i).wait_recv()

    def have_units(first, last):
        for g, group in enumerate(groups):
            if g:
                for u in range(first, last):
                    for n in group[1:]:
                        c_copy(n, u).start()
            for u in range(first, last):
                for n in group:
                    if n != near:
                        c_copy(n, u).wait_recv()

    def add_beta(key, add, k_at=0, k_width=cols):
        depth = pl.ds(k_at, k_width)
        lhs = own if key == 0 else co.at[key - 1]

        @pl.loop(0, cols // tile)
        def _(n):
            at = lanes(n, tile)
            value = product(lhs[:, depth], beta[key, at, depth], 1, 1)
            out[:, at] = out[:, at] + value if add else value

    def term(d, c):
        def one(m):
            return product(ham[m, d], pair[m, :, lanes(c)], 0, 0)

        return one(0) + one(1)

    def add_gathered(m, s, f, b, c):
        at = lanes(c)
        acc[m, :, at] = acc[m, :, at] + product(ham[m, s], ag[f, b, :, at], 1, 0)

    own_load().wait()
    beta_load(0).wait()
    add_beta(0, False)
    pass_piece(0)
    for u in range(1, units // 2 + 1):
        c_copy(groups[0][0], u).start()

    for s in range(line):
        ham_load(s).wait()
    pair_load().wait()

    @pl.loop(0, nc)
    def _(c):
        acc[0, :, lanes(c)] = product(ham[0, z], own[:, lanes(c)], 1, 0)

    for key in range(1, cols_n):
        beta_load(key).wait()
    for u in range(units):
        c_copy(near, u).wait_recv()
    add_beta(1, True)
    have_piece(0)

    def second_products(c):
        at = lanes(c)
        acc[1, :, at] = product(ham[1, z], own[:, at], 1, 0)

        @pl.loop(0, 2)
        def _(f):
            for b in range(2):
                @pl.when(b < place(f))
                def _(b=b):
                    add_gathered(1, turn(place(f) - 1 - b, f), f, b, c)

    for j in range(1, line):
        if j == 2:
            have_units(0, units // 2)
            for key in range(2, cols_n):
                add_beta(key, True, 0, cols // 2)
            pass_piece(1)
            have_piece(1)

        @pl.loop(0, nc)
        def _(c, j=j):
            if j == 1:
                pair_copy(c).wait_recv()

            @pl.loop(0, 2)
            def _(f):
                at = place(f)

                @pl.when(at >= j)
                def _():
                    gather_copy(f, j - 1, c).wait_recv()

                    if j < line - 1:
                        @pl.when(goes_on(f))
                        def _():
                            gather_copy(f, j, c).start()

                @pl.when(jnp.logical_and(at < j, goes_on(f)))
                def _():
                    value = term(turn(line + at - j, f), c)
                    if j == 1:
                        rs[f, j - 1, :, lanes(c)] = value
                    else:
                        @pl.when(at > 0)
                        def _():
                            sum_copy(f, j - 1, c).wait_recv()
                            rs[f, j - 1, :, lanes(c)] = rs[f, j - 1, :, lanes(c)] + value

                        @pl.when(at == 0)
                        def _():
                            rs[f, j - 1, :, lanes(c)] = value

                    sum_copy(f, j, c).start()

            if j == 2:
                @pl.when(c + 2 < line)
                def _():
                    pass_piece(c + 2)

            if j == 3:
                @pl.when(c == 0)
                def _():
                    have_piece(line - 1)

                second_products(c)

            @pl.loop(0, 2)
            def _(f):
                at = place(f)

                @pl.when(at >= j)
                def _():
                    @pl.loop(0, 1 if j < 3 else PAIR)
                    def _(m):
                        add_gathered(m, turn(at - j, f), f, j - 1, c)

            if j == line - 1:
                other_copy(c).start()

        if j == 2:
            for i in range(nc + 2, line):
                pass_piece(i)
            for u in range(units // 2 + 1, units):
                c_copy(groups[0][0], u).start()
            for i in range(2, line - 1):
                have_piece(i)

    have_units(units // 2, units)
    for key in range(2, cols_n):
        add_beta(key, True, cols // 2, cols // 2)

    @pl.loop(0, nc)
    def _(c):
        at = sum_lanes(c)
        out[:, at] = out[:, at] + term(z, c)

    def finish_sums(c):
        at = sum_lanes(c)

        @pl.loop(0, 2)
        def _(f):
            @pl.when(place(f) > 0)
            def _():
                sum_copy(f, line - 1, c).wait_recv()
                out[:, at] = out[:, at] + rs[f, line - 1, :, lanes(c)]

    def finish_gathered(c):
        at = lanes(c)
        other_copy(c).wait_recv()
        out[:, at] = out[:, at] + (acc[0, :, at] + acc_in[:, at])

    @pl.loop(0, nc - 1)
    def _(c):
        finish_sums(c)

    @pl.loop(0, nc)
    def _(c):
        finish_gathered(c)

    for i in range(line):
        piece_copy(i).wait_send()
        for group in hops(i):
            for n in group:
                p_copy(n, i).wait_send()
    for u in range(units):
        for n in range(len(steps)):
            c_copy(n, u).wait_send()
    for c in range(nc):
        pair_copy(c).wait_send()
        other_copy(c).wait_send()

    finish_sums(nc - 1)

    @pl.loop(0, 2)
    def _(f):
        @pl.when(goes_on(f))
        def _():
            @pl.loop(0, nc)
            def _(c):
                for j in range(line):
                    if j < line - 1:
                        @pl.when(j <= place(f))
                        def _(j=j):
                            gather_copy(f, j, c).wait_send()

                    if j:
                        @pl.when(j > place(f))
                        def _(j=j):
                            sum_copy(f, j, c).wait_send()


def solution(mesh):
    line, cols_n = mesh.shape["row"] // PAIR, mesh.shape["col"]
    n_steps = len(exchanges(cols_n))

    def local(coeffs, ham_alpha, ham_beta):
        rows, cols = coeffs.shape
        half = cols // 2
        cw = min(256, half)
        nc = half // cw
        units = cols // LANES
        f32, dma = jnp.float32, pltpu.SemaphoreType.DMA
        any_spec = pl.BlockSpec(memory_space=pl.ANY)
        return pl.pallas_call(
            functools.partial(kernel, line, cols_n, cw),
            out_shape=pltpu.VMEM((rows, cols), f32),
            in_specs=[any_spec, any_spec, any_spec],
            out_specs=pl.BlockSpec(memory_space=pltpu.VMEM),
            scratch_shapes=[
                pltpu.VMEM((rows, cols), f32),
                pltpu.VMEM((PAIR, line, rows, rows), f32),
                pltpu.VMEM((cols_n, cols, cols), f32),
                pltpu.VMEM((cols_n - 1, rows, cols), f32),
                pltpu.VMEM((2, line - 1, rows, half), f32),
                pltpu.VMEM((2, line, rows, half), f32),
                pltpu.VMEM((PAIR, rows, half), f32),
                pltpu.VMEM((rows, half), f32),
                pltpu.VMEM((PAIR, rows, half), f32),
                dma((2,)),
                dma((line,)),
                dma((cols_n,)),
                dma((2, line - 1, nc)),
                dma((2, line - 1, nc)),
                dma((2, line, nc)),
                dma((2, line, nc)),
                dma((line,)),
                dma((line,)),
                dma((nc,)),
                dma((nc,)),
                dma((nc,)),
                dma((nc,)),
                dma((n_steps, line)),
                dma((n_steps, line)),
                dma((n_steps, units)),
                dma((n_steps, units)),
            ],
            compiler_params=pltpu.CompilerParams(
                collective_id=0, has_side_effects=True, vmem_limit_bytes=58 * 2**20
            ),
        )(coeffs, ham_alpha, ham_beta)

    in_specs = (P("row", "col"), P("row", None), P("col", None))
    return jax.shard_map(
        local, mesh=mesh, in_specs=in_specs, out_specs=P("row", "col"), check_vma=False
    )
```
